32 devices in a mesh: groups: 2 (over x), expert: 16 (over z, y, core).
Axes of the slice: x: 2, y: 2, z: 4, core: 2. Of those that a mesh axis runs over, the one named last changes fastest.
Arguments:
- tokens: bfloat16 [2048, 2048], P(('groups', 'expert')), parts along dimension 0, may hold values from -6 to 6
- expert_ids: int32 [2048, 8], P(('groups', 'expert')), parts along dimension 0, may hold values from 0 to 15, as said below
- gate_weights: float32 [2048, 8], P(('groups', 'expert')), parts along dimension 0, may hold values from 0.05 to 0.5
- w_gate: bfloat16 [16, 2048, 768], P('expert'), may hold values from -0.125 to 0.125
- w_up: bfloat16 [16, 2048, 768], P('expert'), may hold values from -0.125 to 0.125
- w_down: bfloat16 [16, 768, 2048], P('expert'), may hold values from -0.21875 to 0.21875
Outputs:
- mixed: bfloat16 [2048, 2048], P(('groups', 'expert')), parts along dimension 0
The draws below stay inside these ranges and needn't reach their ends.
There are 2 independent parts, one for each index of `groups`. The reference program is written for one: setup_inputs(seed, part) draws one part's arguments, and reference() takes and returns one part's arrays. A program takes and returns all parts, laid end to end along the dimension named above; an argument that names none is the same for every part. Nothing has to cross between parts.
Inputs may be any that keep to these rules, and one draw needn't show every extreme that they name: `expert_ids`: each token names 8 different experts. Exactly 2 experts are named exactly 64 times by the tokens of every device; every other expert is named at most 28 times by the tokens of one device, and in every draw some such expert is named exactly 28 times by the tokens of every device.
All inputs are finite; a program needn't handle non-finite values.
Results may differ from the reference program's by a relative error of at most 0.0057.
Values may be sent and summed in bfloat16 or wider, within the bound.
A program may use at most 128 MiB of HBM per device.

```python
import math
from functools import partial
import jax
import jax.numpy as jnp
from jax import lax

D = 2048
FF = 768
TOP = 8
HOT = 2
TOK_DEV = 64
EXPERTS = 16
TOKENS = 1024
CAP = 64


def route_block(is_hot, base_load, extra_load, block_key):
    order_key, token_key, turn_key = jax.random.split(block_key, 3)
    shuffled = jax.random.permutation(order_key, EXPERTS).astype(jnp.int32)
    ranking = jnp.argsort(jnp.argsort(shuffled + EXPERTS * is_hot))
    expert_load = jnp.where(is_hot > 0, CAP, base_load + (ranking < extra_load).astype(jnp.int32))
    load_ends = jnp.cumsum(expert_load)
    slot_index = jnp.arange(TOK_DEV * TOP, dtype=jnp.int32)
    listing = jnp.sum((load_ends[None, :] <= slot_index[:, None]).astype(jnp.int32), axis=1)
    route_table = listing.reshape(TOP, TOK_DEV).T
    rotation = jax.random.randint(turn_key, (TOK_DEV, 1), 0, TOP)
    column = (jnp.arange(TOP, dtype=jnp.int32)[None, :] + rotation) % TOP
    route_table = jnp.take_along_axis(route_table, column, axis=1)
    return route_table[jax.random.permutation(token_key, TOK_DEV)]


def draw_expert_ids(key, part):
    hot_order = jax.random.permutation(jax.random.fold_in(key, 11), EXPERTS)
    is_hot = (hot_order < HOT).astype(jnp.int32)
    spread_rows = TOK_DEV * TOP - HOT * CAP
    base_load = spread_rows // (EXPERTS - HOT)
    extra_load = spread_rows % (EXPERTS - HOT)
    block_keys = jax.random.split(jax.random.fold_in(key, 23), TOKENS // TOK_DEV)
    routed = jax.vmap(partial(route_block, is_hot, base_load, extra_load))(block_keys)
    return routed.reshape(TOKENS, TOP).astype(jnp.int32)


def steps_of(own_key, shape, shards, least, top_value):
    loudness, own = 1.0, jax.random.fold_in(own_key, 6)
    for axis_at, parts in shards:
        steps = jnp.exp(jax.random.uniform(jax.random.fold_in(own, axis_at), (parts,), jnp.float32, least / len(shards), top_value / len(shards)))
        loudness = loudness * jnp.repeat(steps, shape[axis_at] // parts).reshape([-1 if axis == axis_at else 1 for axis in range(len(shape))])
    return loudness


def noise(rng, dims, width, most, cuts=(), kind=jnp.bfloat16):
    array = width * jax.random.normal(rng, dims, jnp.float32)
    if cuts:
        array = array * steps_of(rng, dims, cuts, -0.22, 0.18)
    return jnp.clip(array, -most, most).astype(kind)


def setup_inputs(seed: int = 0, part: int = 0) -> dict:
    key_of = jax.random.split(jax.random.key(seed), 7)
    part_keys = jax.random.split(jax.random.fold_in(key_of[6], part), 7)
    return {
        "tokens": noise(part_keys[0], (TOKENS, D), 1.0, 6.0, ((0, 16),)),
        "expert_ids": draw_expert_ids(jax.random.fold_in(jax.random.fold_in(key_of[6], part), 71), part),
        "gate_weights": jnp.clip(jnp.exp(math.log(0.5) - 2.3025851 * jax.random.uniform(part_keys[2], (TOKENS, TOP), jnp.float32) ** steps_of(part_keys[2], (TOKENS, TOP), ((0, 16),), -0.2, 0.2)), 0.05, 0.5),
        "w_gate": noise(key_of[3], (EXPERTS, D, FF), D ** -0.5, 0.125, ((0, 16),)),
        "w_up": noise(key_of[4], (EXPERTS, D, FF), D ** -0.5, 0.125, ((0, 16),)),
        "w_down": noise(key_of[5], (EXPERTS, FF, D), FF ** -0.5, 0.21875, ((0, 16),)),
    }


row_block = 128


def reference(tokens, expert_ids, gate_weights, w_gate, w_up, w_down):
    flat_ids = expert_ids.reshape(-1).astype(jnp.int32)
    slot_total = flat_ids.shape[0]
    block_count = (slot_total + row_block - 1) // row_block + EXPERTS
    total_rows = block_count * row_block
    expert_range = jnp.arange(EXPERTS, dtype=jnp.int32)
    onehot = (flat_ids[:, None] == expert_range[None, :]).astype(jnp.int32)
    per_expert = jnp.sum(onehot, axis=0)
    rank_inside = jnp.sum(jnp.cumsum(onehot, axis=0) * onehot, axis=1) - 1
    padded_count = (per_expert + row_block - 1) // row_block * row_block
    expert_start = jnp.cumsum(padded_count) - padded_count
    position = expert_start[flat_ids] + rank_inside
    token_of_slot = jnp.arange(slot_total, dtype=jnp.int32) // TOP
    source_token = jnp.full((total_rows,), -1, jnp.int32).at[position].set(token_of_slot)
    block_start = jnp.arange(block_count, dtype=jnp.int32) * row_block
    expert_end = expert_start + padded_count
    block_expert = jnp.sum((expert_end[None, :] <= block_start[:, None]).astype(jnp.int32), axis=1)
    block_expert = jnp.minimum(block_expert, EXPERTS - 1).astype(jnp.int32)

    def one_block(carry, block_pair):
        expert_now, token_slice = block_pair
        is_valid = token_slice >= 0
        picked = tokens[jnp.maximum(token_slice, 0)]
        picked = jnp.where(is_valid[:, None], picked, jnp.zeros((), tokens.dtype))
        gate_part = jnp.dot(picked, w_gate[expert_now], preferred_element_type=jnp.float32)
        up_part = jnp.dot(picked, w_up[expert_now], preferred_element_type=jnp.float32)
        hidden = (jax.nn.silu(gate_part) * up_part).astype(jnp.bfloat16)
        result = jnp.dot(hidden, w_down[expert_now], preferred_element_type=jnp.float32).astype(jnp.bfloat16)
        return carry, result

    carry_out, outputs = lax.scan(one_block, jnp.zeros((), jnp.int32), (block_expert, source_token.reshape(block_count, row_block)))
    expert_out = outputs.reshape(total_rows, D)[position].reshape(TOKENS, TOP, D)
    mixed = jnp.sum(expert_out.astype(jnp.float32) * gate_weights.astype(jnp.float32)[:, :, None], axis=1)
    return mixed.astype(jnp.bfloat16)
```

```python
import functools
import jax
import jax.numpy as jnp
from jax import lax
from jax.experimental import pallas as pl
from jax.experimental.pallas import tpu as pltpu
from jax.sharding import PartitionSpec as P

row_block = 256
pieces = 2
hidden_tile = 256
out_tile = 512
vmem_budget = 48 * 2**20


def swiglu_rows(rows_in, weights):
    gate_part = jnp.dot(rows_in, weights[0], preferred_element_type=jnp.float32)
    up_part = jnp.dot(rows_in, weights[1], preferred_element_type=jnp.float32)
    hidden = (jax.nn.silu(gate_part) * up_part).astype(jnp.bfloat16)
    return jnp.dot(hidden, weights[2], preferred_element_type=jnp.float32).astype(jnp.bfloat16)


def run_blocks(source_rows, block_total, weights, results):

    def block_step(block_num, current):
        row_start = block_num * row_block
        rows_in = lax.dynamic_slice_in_dim(source_rows, row_start, row_block, 0)
        return lax.dynamic_update_slice_in_dim(current, swiglu_rows(rows_in, weights), row_start, 0)

    return lax.fori_loop(jnp.zeros((), jnp.int32), block_total, block_step, results)


def route_and_run(tokens, flat_ids, slot_rank, routed, capacity, device_count, own_weights):
    local_tokens, model_width = tokens.shape
    slot_total = flat_ids.shape[0]
    top_count = slot_total // local_tokens
    buffer_rows = device_count * capacity
    padded_rows = (buffer_rows + row_block - 1) // row_block * row_block
    send_slot = jnp.where(routed, flat_ids * capacity + slot_rank, buffer_rows)
    token_of_slot = jnp.arange(slot_total, dtype=jnp.int32) // top_count
    source_row = jnp.zeros((buffer_rows,), jnp.int32).at[send_slot].set(token_of_slot, mode="drop")
    slot_filled = jnp.zeros((buffer_rows,), jnp.int32).at[send_slot].set(1, mode="drop")
    send_counts = jnp.sum(slot_filled.reshape(device_count, capacity), axis=1)
    outgoing = jnp.where(slot_filled[:, None] > 0, tokens[source_row], jnp.zeros((), jnp.bfloat16))
    outgoing = outgoing.reshape(device_count, capacity, model_width)
    count_column = send_counts.astype(jnp.bfloat16).reshape(device_count, 1)
    incoming, arrived = (
        lax.all_to_all(outgoing, "expert", split_axis=0, concat_axis=0, tiled=True),
        lax.all_to_all(count_column, "expert", split_axis=0, concat_axis=0, tiled=True),
    )
    arrived_counts = arrived.reshape(-1).astype(jnp.int32)
    offsets = jnp.cumsum(arrived_counts) - arrived_counts
    live_total = jnp.sum(arrived_counts)
    slot_index = jnp.arange(buffer_rows, dtype=jnp.int32)
    source_of = slot_index // capacity
    within = slot_index % capacity
    is_live = within < arrived_counts[source_of]
    packed_pos = offsets[source_of] + within
    target_pos = jnp.where(is_live, packed_pos, padded_rows)
    compact_source = (
        jnp.full((padded_rows,), buffer_rows, jnp.int32).at[target_pos].set(slot_index, mode="drop")
    )
    flat_incoming = jnp.concatenate(
        [incoming.reshape(buffer_rows, model_width), jnp.zeros((1, model_width), jnp.bfloat16)],
        axis=0,
    )
    compact = flat_incoming[compact_source]
    block_need = (live_total + row_block - 1) // row_block
    results = run_blocks(
        compact, block_need, own_weights, jnp.zeros((padded_rows, model_width), jnp.bfloat16)
    )
    back_slots = results[jnp.where(is_live, packed_pos, 0)]
    back_slots = jnp.where(is_live[:, None], back_slots, jnp.zeros((), jnp.bfloat16))
    back_slots = back_slots.reshape(device_count, capacity, model_width)
    returned_rows = lax.all_to_all(back_slots, "expert", split_axis=0, concat_axis=0, tiled=True)
    picked = returned_rows.reshape(buffer_rows, model_width)[jnp.where(routed, send_slot, 0)]
    return jnp.where(routed[:, None], picked, jnp.zeros((), jnp.bfloat16))


def visit_order(depth, place):
    return sorted(range(depth), key=lambda g: (abs(g - place), g if 2 * place < depth else -g))


def fused_kernel(
    depth, x_hbm, t_hbm, wg_hbm, wu_hbm, wd_hbm, out_ref,
    rows, tiles, wg, wu, wd, hid, part, a_in, y_out, y_in, c_out, c_in, acc,
    w_sem, own_sem, sx, rx, st, rt, sa, ra, sy, ry, sc, rc,
):
    f32, bf16 = jnp.float32, jnp.bfloat16
    local, width = x_hbm.shape
    inner = wg.shape[1]
    me = lax.axis_index("expert")
    c = lax.rem(me, 2)
    y = lax.rem(me // 2, 2)
    z = me // 4
    own_slot = y * 2 + c
    group_of = []
    for step in range(depth):
        g = jnp.int32(0)
        for place in range(depth):
            g = g + jnp.where(z == place, visit_order(depth, place)[step], 0)
        group_of.append(g)
    sibling = {"expert": (z * 2 + y) * 2 + (1 - c)}
    across = {"expert": (z * 2 + (1 - y)) * 2 + c}

    def along(place):
        return {"expert": (place * 2 + y) * 2 + c}

    has_up, has_down = z < depth - 1, z > 0

    def signal(target):
        pl.semaphore_signal(barrier, inc=1, device_id=target, device_id_type=pl.DeviceIdType.MESH)

    barrier = pltpu.get_barrier_semaphore()
    signal(sibling)
    signal(across)
    pl.when(has_up)(lambda: signal(along(z + 1)))
    pl.when(has_down)(lambda: signal(along(z - 1)))
    pl.semaphore_wait(barrier, 2 + has_up.astype(jnp.int32) + has_down.astype(jnp.int32))

    def remote(src, dst, send, recv, target):
        return pltpu.make_async_remote_copy(
            src_ref=src, dst_ref=dst, send_sem=send, recv_sem=recv,
            device_id=target, device_id_type=pl.DeviceIdType.MESH,
        )

    pending = []

    def launch(copies, cond=None):
        def go():
            for copy in copies:
                copy.start()
        if cond is None:
            go()
        else:
            pl.when(cond)(go)
        pending.append((copies, cond))

    def block_copies(g, slot, src_x, src_t, at, target):
        return [
            remote(src_t, tiles.at[g, slot], st.at[at], rt.at[g, slot], target),
            remote(src_x, rows.at[g, slot], sx.at[at], rx.at[g, slot], target),
        ]

    def push(g, slot, at, target, cond=None):
        launch(block_copies(g, slot, rows.at[g, slot], tiles.at[g, slot], at, target), cond)

    def arrive(g, slot):
        for copy in block_copies(g, slot, rows.at[g, slot], tiles.at[g, slot], 0, sibling):
            copy.wait_recv()

    y_base, c_base = depth + 1, 2 * depth + 1
    launch(block_copies(z, own_slot, x_hbm, t_hbm, 0, along(z + 1)), has_up)
    launch(block_copies(z, own_slot, x_hbm, t_hbm, 1, along(z - 1)), has_down)
    launch(block_copies(z, own_slot, x_hbm, t_hbm, y_base, across))
    launch(block_copies(z, own_slot, x_hbm, t_hbm, c_base, sibling))
    own_copies = [
        pltpu.make_async_copy(x_hbm, rows.at[z, own_slot], own_sem.at[0]),
        pltpu.make_async_copy(t_hbm, tiles.at[z, own_slot], own_sem.at[1]),
    ]
    weight_copies = [
        pltpu.make_async_copy(wg_hbm.at[0], wg, w_sem.at[0]),
        pltpu.make_async_copy(wu_hbm.at[0], wu, w_sem.at[1]),
        pltpu.make_async_copy(wd_hbm.at[0], wd, w_sem.at[2]),
    ]
    for copy in own_copies + weight_copies:
        copy.start()

    def relay_chain(step):
        g = group_of[step]
        arrive(g, own_slot)
        onward = jnp.where(g < z, z + 1, z - 1)
        push(g, own_slot, 1 + step, along(onward), (onward >= 0) & (onward < depth))
        push(g, own_slot, y_base + step, across)
        push(g, own_slot, c_base + step, sibling)

    def relay_across(step):
        g = group_of[step]
        slot = (1 - y) * 2 + c
        arrive(g, slot)
        push(g, slot, c_base + depth + step, sibling)
        arrive(g, y * 2 + 1 - c)
        arrive(g, (1 - y) * 2 + 1 - c)

    def piece_of(p):
        return pl.ds(p * (width // pieces), width // pieces)

    def pair_copy(step, half, p):
        g = group_of[step]
        return remote(
            part.at[g, half * 2 + 1 - c, :, piece_of(p)], a_in.at[g, half, :, piece_of(p)],
            sa.at[step, half, p], ra.at[step, half, p], sibling,
        )

    def run_group(step):
        g = group_of[step]

        def hidden_step(j, carry):
            cols = pl.ds(pl.multiple_of(j * hidden_tile, hidden_tile), hidden_tile)
            block = rows[g].reshape(4 * local, width)
            gate = jnp.dot(block, wg[:, cols], preferred_element_type=f32)
            up = jnp.dot(block, wu[:, cols], preferred_element_type=f32)
            hid[:, cols] = (gate / (1.0 + jnp.exp(-gate)) * up).astype(bf16)
            return carry

        lax.fori_loop(0, inner // hidden_tile, hidden_step, 0)
        span = tiles.shape[3]
        lane = lax.broadcasted_iota(jnp.int32, (local, span), 1)
        line = lax.broadcasted_iota(jnp.int32, (local, span), 0)
        diagonal = (lane == line) | (lane == line + local)
        expert_row = lax.broadcasted_iota(jnp.int32, tiles.shape[2:], 0) == me
        scales = []
        for slot in range(4):
            mine = jnp.sum(
                jnp.where(expert_row, tiles[g, slot].astype(f32), 0.0), axis=0, keepdims=True
            )
            spread = jnp.broadcast_to(mine, (local, span))
            scales.append(jnp.sum(jnp.where(diagonal, spread, 0.0), axis=1, keepdims=True))
        for p in range(pieces):

            def out_step(j, carry):
                first = pl.multiple_of(p * (width // pieces) + j * out_tile, out_tile)
                cols = pl.ds(first, out_tile)
                result = jnp.dot(hid[...], wd[:, cols], preferred_element_type=f32)
                for slot in range(4):
                    scaled = result[slot * local : (slot + 1) * local] * scales[slot]
                    part[g, slot, :, cols] = scaled.astype(bf16)
                return carry

            lax.fori_loop(0, width // pieces // out_tile, out_step, 0)
            for half in range(2):
                launch([pair_copy(step, half, p)])

    def pair_sum(g, half, cols):
        return part[g, half * 2 + c, :, cols].astype(f32) + a_in[g, half, :, cols].astype(f32)

    def across_copy(step, p):
        return remote(
            y_out.at[step, :, piece_of(p)], y_in.at[step, :, piece_of(p)],
            sy.at[step, p], ry.at[step, p], across,
        )

    def send_across(step):
        g = group_of[step]
        for p in range(pieces):
            for half in range(2):
                pair_copy(step, half, p).wait_recv()
            y_out[step, :, piece_of(p)] = pair_sum(g, 1 - y, piece_of(p)).astype(bf16)
            launch([across_copy(step, p)])

    def chain_copy(step, way, g, p, target):
        return remote(
            c_out.at[step, :, piece_of(p)], c_in.at[way, g, :, piece_of(p)],
            sc.at[step, p], rc.at[way, g, p], target,
        )

    def add_chain(way, g, p):
        chain_copy(0, way, g, p, sibling).wait_recv()
        acc[...] += c_in[way, g, :, piece_of(p)].astype(f32)

    def send_chain(step):
        g = group_of[step]
        for p in range(pieces):
            cols = piece_of(p)
            across_copy(step, p).wait_recv()
            acc[...] = pair_sum(g, y, cols) + y_in[step, :, cols].astype(f32)
            if step == 0:
                pl.when(has_down)(lambda: add_chain(0, g, p))
                pl.when(has_up)(lambda: add_chain(1, g, p))
                out_ref[:, cols] = acc[...].astype(bf16)
            else:
                way = jnp.where(g > z, 0, 1)
                pl.when(((g > z) & has_down) | ((g < z) & has_up))(lambda: add_chain(way, g, p))
                c_out[step, :, cols] = acc[...].astype(bf16)
                launch([chain_copy(step, way, g, p, along(jnp.where(g > z, z + 1, z - 1)))])

    for copy in own_copies:
        copy.wait()
    for step in range(depth):
        if step + 1 < depth:
            relay_chain(step + 1)
        relay_across(step)
        if step == 0:
            for copy in weight_copies:
                copy.wait()
        if step == depth - 1 and depth > 2:
            send_across(step - 1)
        run_group(step)
    order = [depth - 2, depth - 1] + list(range(depth - 3, -1, -1))
    for step in order[1 if depth > 2 else 0 :]:
        send_across(step)
    for step in order:
        send_chain(step)
    for copies, cond in pending:
        def finish(copies=copies):
            for copy in copies:
                copy.wait_send()
        if cond is None:
            finish()
        else:
            pl.when(cond)(finish)


def fused_layer(tokens, tile, w_gate, w_up, w_down, depth):
    local, width = tokens.shape
    inner = w_gate.shape[2]
    bf16, f32 = jnp.bfloat16, jnp.float32
    dma = pltpu.SemaphoreType.DMA
    anywhere = pl.BlockSpec(memory_space=pl.ANY)
    sends = 4 * depth + 1
    return pl.pallas_call(
        functools.partial(fused_kernel, depth),
        out_shape=jax.ShapeDtypeStruct((local, width), bf16),
        in_specs=[anywhere] * 5,
        out_specs=pl.BlockSpec(memory_space=pltpu.VMEM),
        scratch_shapes=[
            pltpu.VMEM((depth, 4, local, width), bf16),
            pltpu.VMEM((depth, 4) + tile.shape, bf16),
            pltpu.VMEM((width, inner), bf16),
            pltpu.VMEM((width, inner), bf16),
            pltpu.VMEM((inner, width), bf16),
            pltpu.VMEM((4 * local, inner), bf16),
            pltpu.VMEM((depth, 4, local, width), bf16),
            pltpu.VMEM((depth, 2, local, width), bf16),
            pltpu.VMEM((depth, local, width), bf16),
            pltpu.VMEM((depth, local, width), bf16),
            pltpu.VMEM((depth, local, width), bf16),
            pltpu.VMEM((2, depth, local, width), bf16),
            pltpu.VMEM((local, width // pieces), f32),
            dma((3,)), dma((2,)),
            dma((sends,)), dma((depth, 4)), dma((sends,)), dma((depth, 4)),
            dma((depth, 2, pieces)), dma((depth, 2, pieces)),
            dma((depth, pieces)), dma((depth, pieces)),
            dma((depth, pieces)), dma((2, depth, pieces)),
        ],
        compiler_params=pltpu.CompilerParams(
            collective_id=0, has_side_effects=True, vmem_limit_bytes=60 * 2**20
        ),
    )(tokens, tile, w_gate, w_up, w_down)


def choice_tile(expert_ids, gate_weights, expert_total):
    experts = jnp.arange(expert_total, dtype=jnp.int32)[:, None, None]
    chosen = experts == expert_ids[None, :, :]
    dense = jnp.sum(jnp.where(chosen, gate_weights[None, :, :], 0.0), axis=2)
    high = lax.reduce_precision(dense, 8, 7)
    return jnp.concatenate([high, dense - high], axis=1).astype(jnp.bfloat16)


def fits_fused(device_count, local_tokens, model_width, inner):
    gathered = 2 * device_count * local_tokens * model_width
    weights = 6 * model_width * inner
    return (
        device_count % 4 == 0
        and device_count >= 8
        and 2 * local_tokens % 128 == 0
        and model_width % (pieces * out_tile) == 0
        and inner % hidden_tile == 0
        and 4 * gathered + weights <= vmem_budget
    )


def shards(tokens, expert_ids, gate_weights, w_gate, w_up, w_down):
    device_count = lax.axis_size("expert")
    local_tokens, model_width = tokens.shape
    top_count = expert_ids.shape[1]
    expert_total = device_count * w_gate.shape[0]
    capacity = min(
        local_tokens, 4 * ((local_tokens * top_count + expert_total - 1) // expert_total)
    )
    if fits_fused(device_count, local_tokens, model_width, w_gate.shape[2]):
        tile = choice_tile(expert_ids, gate_weights, expert_total)
        return fused_layer(tokens, tile, w_gate, w_up, w_down, device_count // 4)
    flat_ids = expert_ids.reshape(-1)
    slot_total = flat_ids.shape[0]
    expert_range = jnp.arange(device_count, dtype=jnp.int32)
    onehot = (flat_ids[:, None] == expert_range[None, :]).astype(jnp.int32)
    slot_rank = jnp.sum(jnp.cumsum(onehot, axis=0) * onehot, axis=1) - 1
    own_weights = (w_gate[0], w_up[0], w_down[0])
    routed = jnp.ones((slot_total,), jnp.bool_)
    slot_values = route_and_run(
        tokens, flat_ids, slot_rank, routed, capacity, device_count, own_weights
    )
    picked = slot_values.reshape(local_tokens, top_count, model_width)
    mixed = jnp.sum(picked.astype(jnp.float32) * gate_weights[:, :, None], axis=1)
    return mixed.astype(jnp.bfloat16)


def solution(mesh):
    placed = (
        P(("groups", "expert"), None),
        P(("groups", "expert"), None),
        P(("groups", "expert"), None),
        P("expert", None, None),
        P("expert", None, None),
        P("expert", None, None),
    )
    return jax.shard_map(
        shards, mesh=mesh, in_specs=placed, out_specs=P(("groups", "expert"), None), check_vma=False
    )
```

```python
import functools
import jax
import jax.numpy as jnp
from jax import lax
from jax.experimental import pallas as pl
from jax.experimental.pallas import tpu as pltpu
from jax.sharding import PartitionSpec as P

row_block = 256
pieces = 4
chunks = 4
hidden_tile = 256
vmem_budget = 48 * 2**20


def swiglu_rows(rows_in, weights):
    gate_part = jnp.dot(rows_in, weights[0], preferred_element_type=jnp.float32)
    up_part = jnp.dot(rows_in, weights[1], preferred_element_type=jnp.float32)
    hidden = (jax.nn.silu(gate_part) * up_part).astype(jnp.bfloat16)
    return jnp.dot(hidden, weights[2], preferred_element_type=jnp.float32).astype(jnp.bfloat16)


def run_blocks(source_rows, block_total, weights, results):

    def block_step(block_num, current):
        row_start = block_num * row_block
        rows_in = lax.dynamic_slice_in_dim(source_rows, row_start, row_block, 0)
        return lax.dynamic_update_slice_in_dim(current, swiglu_rows(rows_in, weights), row_start, 0)

    return lax.fori_loop(jnp.zeros((), jnp.int32), block_total, block_step, results)


def route_and_run(tokens, flat_ids, slot_rank, routed, capacity, device_count, own_weights):
    local_tokens, model_width = tokens.shape
    slot_total = flat_ids.shape[0]
    top_count = slot_total // local_tokens
    buffer_rows = device_count * capacity
    padded_rows = (buffer_rows + row_block - 1) // row_block * row_block
    send_slot = jnp.where(routed, flat_ids * capacity + slot_rank, buffer_rows)
    token_of_slot = jnp.arange(slot_total, dtype=jnp.int32) // top_count
    source_row = jnp.zeros((buffer_rows,), jnp.int32).at[send_slot].set(token_of_slot, mode="drop")
    slot_filled = jnp.zeros((buffer_rows,), jnp.int32).at[send_slot].set(1, mode="drop")
    send_counts = jnp.sum(slot_filled.reshape(device_count, capacity), axis=1)
    outgoing = jnp.where(slot_filled[:, None] > 0, tokens[source_row], jnp.zeros((), jnp.bfloat16))
    outgoing = outgoing.reshape(device_count, capacity, model_width)
    count_column = send_counts.astype(jnp.bfloat16).reshape(device_count, 1)
    incoming, arrived = (
        lax.all_to_all(outgoing, "expert", split_axis=0, concat_axis=0, tiled=True),
        lax.all_to_all(count_column, "expert", split_axis=0, concat_axis=0, tiled=True),
    )
    arrived_counts = arrived.reshape(-1).astype(jnp.int32)
    offsets = jnp.cumsum(arrived_counts) - arrived_counts
    live_total = jnp.sum(arrived_counts)
    slot_index = jnp.arange(buffer_rows, dtype=jnp.int32)
    source_of = slot_index // capacity
    within = slot_index % capacity
    is_live = within < arrived_counts[source_of]
    packed_pos = offsets[source_of] + within
    target_pos = jnp.where(is_live, packed_pos, padded_rows)
    compact_source = (
        jnp.full((padded_rows,), buffer_rows, jnp.int32).at[target_pos].set(slot_index, mode="drop")
    )
    flat_incoming = jnp.concatenate(
        [incoming.reshape(buffer_rows, model_width), jnp.zeros((1, model_width), jnp.bfloat16)],
        axis=0,
    )
    compact = flat_incoming[compact_source]
    block_need = (live_total + row_block - 1) // row_block
    results = run_blocks(
        compact, block_need, own_weights, jnp.zeros((padded_rows, model_width), jnp.bfloat16)
    )
    back_slots = results[jnp.where(is_live, packed_pos, 0)]
    back_slots = jnp.where(is_live[:, None], back_slots, jnp.zeros((), jnp.bfloat16))
    back_slots = back_slots.reshape(device_count, capacity, model_width)
    returned_rows = lax.all_to_all(back_slots, "expert", split_axis=0, concat_axis=0, tiled=True)
    picked = returned_rows.reshape(buffer_rows, model_width)[jnp.where(routed, send_slot, 0)]
    return jnp.where(routed[:, None], picked, jnp.zeros((), jnp.bfloat16))


def visit_order(depth, place):
    return sorted(range(depth), key=lambda g: (abs(g - place), g if 2 * place < depth else -g))


def fused_kernel(
    depth, x_hbm, t_hbm, wg_hbm, wu_hbm, wd_hbm, out_ref,
    rows, tiles, wg, wu, wd, hid, part, a_in, y_out, y_in, c_out, c_in, acc,
    w_sem, own_sem, sx, rx, st, rt, sa, ra, sy, ry, sc, rc,
):
    f32, bf16 = jnp.float32, jnp.bfloat16
    local, width = x_hbm.shape
    inner = wg.shape[1]
    me = lax.axis_index("expert")
    c = lax.rem(me, 2)
    y = lax.rem(me // 2, 2)
    z = me // 4
    own_slot = y * 2 + c
    group_of = []
    for step in range(depth):
        g = jnp.int32(0)
        for place in range(depth):
            g = g + jnp.where(z == place, visit_order(depth, place)[step], 0)
        group_of.append(g)
    sibling = {"expert": (z * 2 + y) * 2 + (1 - c)}
    across = {"expert": (z * 2 + (1 - y)) * 2 + c}

    def along(place):
        return {"expert": (place * 2 + y) * 2 + c}

    has_up, has_down = z < depth - 1, z > 0

    def signal(target):
        pl.semaphore_signal(barrier, inc=1, device_id=target, device_id_type=pl.DeviceIdType.MESH)

    barrier = pltpu.get_barrier_semaphore()
    signal(sibling)
    signal(across)
    pl.when(has_up)(lambda: signal(along(z + 1)))
    pl.when(has_down)(lambda: signal(along(z - 1)))
    pl.semaphore_wait(barrier, 2 + has_up.astype(jnp.int32) + has_down.astype(jnp.int32))

    def remote(src, dst, send, recv, target):
        return pltpu.make_async_remote_copy(
            src_ref=src, dst_ref=dst, send_sem=send, recv_sem=recv,
            device_id=target, device_id_type=pl.DeviceIdType.MESH,
        )

    pending = []

    def launch(copies, cond=None):
        def go():
            for copy in copies:
                copy.start()
        if cond is None:
            go()
        else:
            pl.when(cond)(go)
        pending.append((copies, cond))

    chunk_rows = local // chunks

    def chunk_copies(g, slot, h, src_x, src_t, at, target):
        part_rows = pl.ds(h * chunk_rows, chunk_rows)
        copies = [
            remote(
                src_x.at[part_rows], rows.at[g, slot, part_rows],
                sx.at[at, h], rx.at[g, slot, h], target,
            )
        ]
        if h == 0:
            copies.append(remote(src_t, tiles.at[g, slot], st.at[at], rt.at[g, slot], target))
        return copies

    def push(g, slot, h, at, target, cond=None):
        launch(chunk_copies(g, slot, h, rows.at[g, slot], tiles.at[g, slot], at, target), cond)

    def arrive(g, slot, h):
        for copy in chunk_copies(g, slot, h, rows.at[g, slot], tiles.at[g, slot], 0, sibling):
            copy.wait_recv()

    y_base, c_base = depth + 1, 2 * depth + 1
    for h in range(chunks):
        launch(chunk_copies(z, own_slot, h, x_hbm, t_hbm, 0, along(z + 1)), has_up)
        launch(chunk_copies(z, own_slot, h, x_hbm, t_hbm, 1, along(z - 1)), has_down)
        launch(chunk_copies(z, own_slot, h, x_hbm, t_hbm, y_base, across))
    for h in range(chunks):
        launch(chunk_copies(z, own_slot, h, x_hbm, t_hbm, c_base, sibling))
    own_copies = [
        pltpu.make_async_copy(x_hbm, rows.at[z, own_slot], own_sem.at[0]),
        pltpu.make_async_copy(t_hbm, tiles.at[z, own_slot], own_sem.at[1]),
    ]
    weight_copies = [
        pltpu.make_async_copy(wg_hbm.at[0], wg, w_sem.at[0]),
        pltpu.make_async_copy(wu_hbm.at[0], wu, w_sem.at[1]),
        pltpu.make_async_copy(wd_hbm.at[0], wd, w_sem.at[2]),
    ]
    for copy in own_copies + weight_copies:
        copy.start()

    def relay_chain(step, h):
        g = group_of[step]
        arrive(g, own_slot, h)
        onward = jnp.where(g < z, z + 1, z - 1)
        push(g, own_slot, h, 1 + step, along(onward), (onward >= 0) & (onward < depth))
        push(g, own_slot, h, y_base + step, across)
        push(g, own_slot, h, c_base + step, sibling)

    def relay_across(step, h):
        g = group_of[step]
        slot = (1 - y) * 2 + c
        arrive(g, slot, h)
        push(g, slot, h, c_base + depth + step, sibling)

    def await_sibling(step):
        g = group_of[step]
        for h in range(chunks):
            arrive(g, y * 2 + 1 - c, h)
            arrive(g, (1 - y) * 2 + 1 - c, h)

    def piece_of(p):
        return pl.ds(p * (width // pieces), width // pieces)

    def pair_copy(step, half, p):
        g = group_of[step]
        return remote(
            part.at[g, half * 2 + 1 - c, :, piece_of(p)], a_in.at[g, half, :, piece_of(p)],
            sa.at[step, half, p], ra.at[step, half, p], sibling,
        )

    def run_hidden(step, j):
        g = group_of[step]
        cols = pl.ds(j * hidden_tile, hidden_tile)
        block = rows[g].reshape(4 * local, width)
        gate = jnp.dot(block, wg[:, cols], preferred_element_type=f32)
        up = jnp.dot(block, wu[:, cols], preferred_element_type=f32)
        hid[:, cols] = (gate / (1.0 + jnp.exp(-gate)) * up).astype(bf16)

    def run_out(step):
        g = group_of[step]
        span = tiles.shape[3]
        lane = lax.broadcasted_iota(jnp.int32, (local, span), 1)
        line = lax.broadcasted_iota(jnp.int32, (local, span), 0)
        diagonal = (lane == line) | (lane == line + local)
        expert_row = lax.broadcasted_iota(jnp.int32, tiles.shape[2:], 0) == me
        scales = []
        for slot in range(4):
            mine = jnp.sum(
                jnp.where(expert_row, tiles[g, slot].astype(f32), 0.0), axis=0, keepdims=True
            )
            spread = jnp.broadcast_to(mine, (local, span))
            scales.append(jnp.sum(jnp.where(diagonal, spread, 0.0), axis=1, keepdims=True))
        for p in range(pieces):
            cols = piece_of(p)
            result = jnp.dot(hid[...], wd[:, cols], preferred_element_type=f32)
            for slot in range(4):
                scaled = result[slot * local : (slot + 1) * local] * scales[slot]
                part[g, slot, :, cols] = scaled.astype(bf16)
            for half in range(2):
                launch([pair_copy(step, half, p)])

    hidden_total = inner // hidden_tile

    def run_part(step, h):
        if h == 0:
            await_sibling(step)
            if step == 0:
                for copy in own_copies + weight_copies:
                    copy.wait()
        for j in range(hidden_total):
            if j * (chunks - 1) // hidden_total == h:
                run_hidden(step, j)
        if h == chunks - 1:
            run_out(step)

    def pair_sum(g, half, cols):
        return part[g, half * 2 + c, :, cols].astype(f32) + a_in[g, half, :, cols].astype(f32)

    def across_copy(step, p):
        return remote(
            y_out.at[step, :, piece_of(p)], y_in.at[step, :, piece_of(p)],
            sy.at[step, p], ry.at[step, p], across,
        )

    def send_across(step):
        g = group_of[step]
        for p in range(pieces):
            for half in range(2):
                pair_copy(step, half, p).wait_recv()
            y_out[step, :, piece_of(p)] = pair_sum(g, 1 - y, piece_of(p)).astype(bf16)
            launch([across_copy(step, p)])

    def chain_copy(step, way, g, p, target):
        return remote(
            c_out.at[step, :, piece_of(p)], c_in.at[way, g, :, piece_of(p)],
            sc.at[step, p], rc.at[way, g, p], target,
        )

    def add_chain(way, g, p):
        chain_copy(0, way, g, p, sibling).wait_recv()
        acc[...] += c_in[way, g, :, piece_of(p)].astype(f32)

    def send_chain(step):
        g = group_of[step]
        for p in range(pieces):
            cols = piece_of(p)
            across_copy(step, p).wait_recv()
            acc[...] = pair_sum(g, y, cols) + y_in[step, :, cols].astype(f32)
            if step == 0:
                pl.when(has_down)(lambda: add_chain(0, g, p))
                pl.when(has_up)(lambda: add_chain(1, g, p))
                out_ref[:, cols] = acc[...].astype(bf16)
            else:
                way = jnp.where(g > z, 0, 1)
                pl.when(((g > z) & has_down) | ((g < z) & has_up))(lambda: add_chain(way, g, p))
                c_out[step, :, cols] = acc[...].astype(bf16)
                launch([chain_copy(step, way, g, p, along(jnp.where(g > z, z + 1, z - 1)))])

    for turn in range(1, depth + 1):
        for h in range(chunks):
            if turn < depth:
                relay_chain(turn, h)
            relay_across(turn - 1, h)
            if turn >= 2:
                run_part(turn - 2, h)
    if depth > 2:
        send_across(depth - 2)
    for h in range(chunks):
        run_part(depth - 1, h)
    order = [depth - 2, depth - 1] + list(range(depth - 3, -1, -1))
    for step in order[1 if depth > 2 else 0 :]:
        send_across(step)
    for step in order:
        send_chain(step)
    for copies, cond in pending:
        def finish(copies=copies):
            for copy in copies:
                copy.wait_send()
        if cond is None:
            finish()
        else:
            pl.when(cond)(finish)


def fused_layer(tokens, tile, w_gate, w_up, w_down, depth):
    local, width = tokens.shape
    inner = w_gate.shape[2]
    bf16, f32 = jnp.bfloat16, jnp.float32
    dma = pltpu.SemaphoreType.DMA
    anywhere = pl.BlockSpec(memory_space=pl.ANY)
    sends = 4 * depth + 1
    return pl.pallas_call(
        functools.partial(fused_kernel, depth),
        out_shape=jax.ShapeDtypeStruct((local, width), bf16),
        in_specs=[anywhere] * 5,
        out_specs=pl.BlockSpec(memory_space=pltpu.VMEM),
        scratch_shapes=[
            pltpu.VMEM((depth, 4, local, width), bf16),
            pltpu.VMEM((depth, 4) + tile.shape, bf16),
            pltpu.VMEM((width, inner), bf16),
            pltpu.VMEM((width, inner), bf16),
            pltpu.VMEM((inner, width), bf16),
            pltpu.VMEM((4 * local, inner), bf16),
            pltpu.VMEM((depth, 4, local, width), bf16),
            pltpu.VMEM((depth, 2, local, width), bf16),
            pltpu.VMEM((depth, local, width), bf16),
            pltpu.VMEM((depth, local, width), bf16),
            pltpu.VMEM((depth, local, width), bf16),
            pltpu.VMEM((2, depth, local, width), bf16),
            pltpu.VMEM((local, width // pieces), f32),
            dma((3,)), dma((2,)),
            dma((sends, chunks)), dma((depth, 4, chunks)), dma((sends,)), dma((depth, 4)),
            dma((depth, 2, pieces)), dma((depth, 2, pieces)),
            dma((depth, pieces)), dma((depth, pieces)),
            dma((depth, pieces)), dma((2, depth, pieces)),
        ],
        compiler_params=pltpu.CompilerParams(
            collective_id=0, has_side_effects=True, vmem_limit_bytes=60 * 2**20
        ),
    )(tokens, tile, w_gate, w_up, w_down)


def choice_tile(expert_ids, gate_weights, expert_total):
    experts = jnp.arange(expert_total, dtype=jnp.int32)[:, None, None]
    chosen = experts == expert_ids[None, :, :]
    dense = jnp.sum(jnp.where(chosen, gate_weights[None, :, :], 0.0), axis=2)
    high = lax.reduce_precision(dense, 8, 7)
    return jnp.concatenate([high, dense - high], axis=1).astype(jnp.bfloat16)


def fits_fused(device_count, local_tokens, model_width, inner):
    gathered = 2 * device_count * local_tokens * model_width
    weights = 6 * model_width * inner
    return (
        device_count % 4 == 0
        and device_count >= 8
        and 2 * local_tokens % 128 == 0
        and local_tokens % (16 * chunks) == 0
        and model_width % (pieces * 128) == 0
        and inner % hidden_tile == 0
        and 4 * gathered + weights <= vmem_budget
    )


def shards(tokens, expert_ids, gate_weights, w_gate, w_up, w_down):
    device_count = lax.axis_size("expert")
    local_tokens, model_width = tokens.shape
    top_count = expert_ids.shape[1]
    expert_total = device_count * w_gate.shape[0]
    capacity = min(
        local_tokens, 4 * ((local_tokens * top_count + expert_total - 1) // expert_total)
    )
    if fits_fused(device_count, local_tokens, model_width, w_gate.shape[2]):
        tile = choice_tile(expert_ids, gate_weights, expert_total)
        return fused_layer(tokens, tile, w_gate, w_up, w_down, device_count // 4)
    flat_ids = expert_ids.reshape(-1)
    slot_total = flat_ids.shape[0]
    expert_range = jnp.arange(device_count, dtype=jnp.int32)
    onehot = (flat_ids[:, None] == expert_range[None, :]).astype(jnp.int32)
    slot_rank = jnp.sum(jnp.cumsum(onehot, axis=0) * onehot, axis=1) - 1
    own_weights = (w_gate[0], w_up[0], w_down[0])
    routed = jnp.ones((slot_total,), jnp.bool_)
    slot_values = route_and_run(
        tokens, flat_ids, slot_rank, routed, capacity, device_count, own_weights
    )
    picked = slot_values.reshape(local_tokens, top_count, model_width)
    mixed = jnp.sum(picked.astype(jnp.float32) * gate_weights[:, :, None], axis=1)
    return mixed.astype(jnp.bfloat16)


def solution(mesh):
    placed = (
        P(("groups", "expert"), None),
        P(("groups", "expert"), None),
        P(("groups", "expert"), None),
        P("expert", None, None),
        P("expert", None, None),
        P("expert", None, None),
    )
    return jax.shard_map(
        shards, mesh=mesh, in_specs=placed, out_specs=P(("groups", "expert"), None), check_vma=False
    )
```
